32 devices in a mesh: region: 2 (over x), row: 4 (over z), col: 4 (over y, core).
Axes of the slice: x: 2, y: 2, z: 4, core: 2. Of those that a mesh axis runs over, the one named last changes fastest.
Arguments:
- covariance: float32 [8, 4096, 4096], P('region', 'row', 'col'), parts along dimension 0, as said below
- prior: float32 [16, 3, 256, 256], P('col'), may hold values from -0.21875 to 0.21875
- offsets: int32 [16, 3], replicated, may hold values from 0 to 15, as said below
- basis: float32 [8, 4096, 64], P('region', 'col'), parts along dimension 0, may hold values from -6 to 6
Outputs:
- whitened: float32 [8, 4096, 4096], P('region', 'row', 'col'), parts along dimension 0
- foreground_basis: float32 [8, 4096, 64], P('region', 'col'), parts along dimension 0
The draws below stay inside these ranges and needn't reach their ends.
There are 2 independent parts, one for each index of `region`. The reference program is written for one: setup_inputs(seed, part) draws one part's arguments, and reference() takes and returns one part's arrays. A program takes and returns all parts, laid end to end along the dimension named above; an argument that names none is the same for every part. Nothing has to cross between parts.
Inputs may be any that keep to these rules, and one draw needn't show every extreme that they name: Row i of offsets begins with i; its other entries are distinct tile rows other than i, each within 2 of i. covariance is exactly symmetric in its last two dimensions.
All inputs are finite; a program needn't handle non-finite values.
Results may differ from the reference program's by a relative error of at most 0.0003.
Values sent between devices are 32-bit elements; how exact they have to be, the bound alone decides.
A program may use at most 320 MiB of HBM per device.

```python
import math
import jax
import jax.numpy as jnp
from jax import lax

NCH = 4096
TILE = 256
BAND = 3
H = 2
K = 64
S = 4
ITERS = 2
NB = 16


def draw_covariance(key, part):
    key_scale, key_noise = jax.random.split(key)
    ceiling = 10.0
    noise_draw = jax.random.normal(key_noise, (S, NCH, NCH), jnp.float32)
    spread = jnp.exp(jax.random.uniform(key_scale, (S, NCH), jnp.float32, 0.0, 1.0) * math.log(ceiling))
    symmetric = (noise_draw + jnp.swapaxes(noise_draw, 1, 2)) * (1.0 / math.sqrt(2.0 * NCH))
    outer_scale = spread[:, :, None] * spread[:, None, :]
    diagonal = jnp.eye(NCH, dtype=jnp.float32)[None] * (spread * spread)[:, :, None]
    return outer_scale * symmetric + diagonal


def draw_offsets(key, part):
    row_index = jnp.arange(NB, dtype=jnp.int32)[:, None]
    slot_index = jnp.arange(2 * H, dtype=jnp.int32)
    distance = jnp.where(slot_index < H, slot_index - H, slot_index - H + 1)
    candidates = row_index + distance[None, :]
    inside = (candidates >= 0) & (candidates < NB)
    priority = jax.random.randint(key, (NB, 2 * H), 0, 1024, dtype=jnp.int32) * (2 * H) + slot_index[None, :]
    priority = jnp.where(inside, priority, jnp.int32(1 << 30))
    ranking = jnp.argsort(priority, axis=1)
    chosen = jnp.take_along_axis(candidates, ranking[:, :BAND - 1], axis=1)
    return jnp.concatenate([row_index, chosen], axis=1).astype(jnp.int32)


def shard_levels(rng, extent, cuts, least, high):
    level = 1.0
    for axis_at, shards_of in cuts:
        heights = jax.random.uniform(jax.random.fold_in(jax.random.fold_in(rng, 6), axis_at), (shards_of,), jnp.float32, least / len(cuts), high / len(cuts))
        level = level * jnp.repeat(jnp.exp(heights), extent[axis_at] // shards_of).reshape((-1,) + (1,) * (len(extent) - 1 - axis_at))
    return level


def normal_values(own_key, extent, scale, most, shards=(), held_as=jnp.bfloat16):
    loudness = shard_levels(own_key, extent, shards, -0.22, 0.18) if shards else 1.0
    array = jax.random.normal(own_key, extent, jnp.float32) * scale * loudness
    return jnp.minimum(jnp.maximum(array, -most), most).astype(held_as)


def setup_inputs(seed: int = 0, part: int = 0) -> dict:
    seeds = jax.random.split(jax.random.key(seed), 5)
    part_keys = jax.random.split(jax.random.fold_in(seeds[4], part), 5)
    return {
        "covariance": draw_covariance(jax.random.fold_in(jax.random.fold_in(seeds[4], part), 71), part),
        "prior": normal_values(seeds[1], (NB, BAND, TILE, TILE), (BAND * TILE) ** -0.5, 0.21875, ((0, 4),), jnp.float32),
        "offsets": draw_offsets(jax.random.fold_in(seeds[4], 71), part),
        "basis": normal_values(part_keys[3], (S, NCH, K), 1.0, 6.0, ((1, 4),), jnp.float32),
    }


full_precision = lax.Precision.HIGHEST

def left_whiten(matrix, prior, offsets):
    width = matrix.shape[2]
    tiles = matrix.reshape(matrix.shape[0], NB, TILE, width)

    def one_row(index):
        picked = jnp.take(tiles, offsets[index], axis=1)
        return jnp.einsum('bpq,sbqm->spm', prior[index], picked, precision=full_precision)
    rows_out = lax.map(one_row, jnp.arange(NB, dtype=jnp.int32))
    return jnp.swapaxes(rows_out, 0, 1).reshape(matrix.shape)

def reference(covariance, prior, offsets, basis):
    whitened_left = left_whiten(covariance, prior, offsets)
    whitened = jnp.swapaxes(left_whiten(jnp.swapaxes(whitened_left, 1, 2), prior, offsets), 1, 2)
    current = basis
    for sweep in range(ITERS):
        modes = jnp.einsum('smn,snk->smk', whitened, current, precision=full_precision)
        gram = jnp.einsum('snk,snl->skl', modes, modes, precision=full_precision)
        lower = jnp.linalg.cholesky(gram)
        current = lax.linalg.triangular_solve(lower, modes, left_side=False, lower=True, transpose_a=True)
    return (whitened, current)
```

```python
import functools
import jax
import jax.numpy as jnp
from jax import lax
from jax.experimental import pallas as pl
from jax.experimental.pallas import tpu as pltpu
from jax.sharding import PartitionSpec as P

H = 2
ITERS = 2


full_precision = lax.Precision.HIGHEST
MESH = pl.DeviceIdType.MESH
NN = (((1,), (0,)), ((), ()))
NT = (((1,), (1,)), ((), ()))


def halos(array, axis, dim, width):
    peers, length = lax.axis_size(axis), array.shape[dim]
    before, after = [], []
    done, step = 0, 1
    while done < width:
        take = min(length, width - done)
        last = lax.slice_in_dim(array, length - take, length, axis=dim)
        lead = lax.slice_in_dim(array, 0, take, axis=dim)
        before.insert(0, lax.ppermute(last, axis, [(i, i + step) for i in range(peers - step)]))
        after.append(lax.ppermute(lead, axis, [(i + step, i) for i in range(peers - step)]))
        done, step = done + take, step + 1
    return before, after


def halves(x):
    high = x.astype(jnp.bfloat16)
    return high, (x - high.astype(jnp.float32)).astype(jnp.bfloat16)


def product(a, b, dims):
    ah, al = a
    bh, bl = b
    dot = functools.partial(lax.dot_general, dimension_numbers=dims, preferred_element_type=jnp.float32)
    return dot(ah, bh) + (dot(ah, bl) + dot(al, bh))


def left_kernel(slots, tab_ref, p_ref, *refs):
    out_ref = refs[-1]
    total = None
    for b in range(slots):
        term = product(halves(p_ref[0, b]), halves(refs[b][...]), NN)
        total = term if total is None else total + term
    out_ref[...] = total


def left_whiten(table, prior, padded, rows):
    tiles, slots, tile, _ = prior.shape
    cols = padded.shape[1]

    def band_map(b, i, tab):
        return (tab[i * slots + b], 0)

    return pl.pallas_call(
        functools.partial(left_kernel, slots),
        out_shape=jax.ShapeDtypeStruct((rows, cols), jnp.float32),
        grid_spec=pltpu.PrefetchScalarGridSpec(
            num_scalar_prefetch=1,
            grid=(tiles,),
            in_specs=[pl.BlockSpec((1, slots, tile, tile), lambda i, tab: (i, 0, 0, 0))]
            + [pl.BlockSpec((tile, cols), functools.partial(band_map, b)) for b in range(slots)],
            out_specs=pl.BlockSpec((tile, cols), lambda i, tab: (i, 0)),
        ),
        cost_estimate=pl.CostEstimate(
            flops=6 * rows * slots * tile * cols, bytes_accessed=4 * rows * cols * 4, transcendentals=0
        ),
        name="left_whiten",
    )(table, prior, *([padded] * slots))


def right_kernel(slots, aliased, tab_ref, p_ref, cur_ref, *refs):
    out_ref, modes_ref = refs[slots + aliased], refs[slots + aliased + 1]
    total = None
    for b in range(slots):
        term = product(halves(refs[b][...]), halves(p_ref[0, b]), NT)
        total = term if total is None else total + term
    out_ref[0] = total
    part = product(halves(cur_ref[...]), halves(total), NT)
    step = pl.program_id(0)

    @pl.when(step == 0)
    def _():
        modes_ref[...] = part

    @pl.when(step > 0)
    def _():
        modes_ref[...] += part


def right_whiten(table, prior, widened, current, scale, scales, cols, held):
    tiles, slots, tile, _ = prior.shape
    rows = widened.shape[0]
    modes = current.shape[0]

    def band_map(b, j, tab):
        return (0, tab[j * slots + b])

    aliased = 0 if held is None else 1
    in_specs = [
        pl.BlockSpec((1, slots, tile, tile), lambda j, tab: (j, 0, 0, 0)),
        pl.BlockSpec((modes, tile), lambda j, tab: (0, j)),
    ] + [pl.BlockSpec((rows, tile), functools.partial(band_map, b)) for b in range(slots)]
    args = [table, prior, current] + [widened] * slots
    aliases = {}
    if aliased:
        in_specs.append(pl.BlockSpec(memory_space=pl.ANY))
        aliases = {len(args): 0}
        args.append(held)
    return pl.pallas_call(
        functools.partial(right_kernel, slots, aliased),
        out_shape=(
            jax.ShapeDtypeStruct((scales, rows, cols), jnp.float32),
            jax.ShapeDtypeStruct((modes, rows), jnp.float32),
        ),
        grid_spec=pltpu.PrefetchScalarGridSpec(
            num_scalar_prefetch=1,
            grid=(tiles,),
            in_specs=in_specs,
            out_specs=[
                pl.BlockSpec((1, rows, tile), lambda j, tab: (scale, 0, j)),
                pl.BlockSpec((modes, rows), lambda j, tab: (0, 0)),
            ],
        ),
        input_output_aliases=aliases,
        cost_estimate=pl.CostEstimate(
            flops=6 * rows * slots * tile * cols, bytes_accessed=4 * rows * cols * 4, transcendentals=0
        ),
        name="right_whiten",
    )(*args)


def inverse_factor(gram):
    size = gram.shape[0]
    shape = (size, 2 * size)
    sub = lax.broadcasted_iota(jnp.int32, shape, 0)
    lane = lax.broadcasted_iota(jnp.int32, shape, 1)
    unit = jnp.where(lane == sub + size, 1.0, 0.0).astype(jnp.float32)
    start = jnp.concatenate([gram, unit[:, size:]], axis=1)

    def step(j, a):
        row = jnp.sum(jnp.where(sub == j, a, 0.0), axis=0, keepdims=True)
        col = jnp.sum(jnp.where(lane == j, a, 0.0), axis=1, keepdims=True)
        pivot = jnp.sum(jnp.where(lane[:1] == j, row, 0.0), axis=1, keepdims=True)
        scale = 1.0 / jnp.sqrt(pivot)
        row = row * scale
        return jnp.where(sub == j, row, jnp.where(sub > j, a - (col * scale) * row, a))

    return lax.fori_loop(0, size, step, start)[:, size:]


def reduce_kernel(axis, other, n, m, x_ref, out_ref, parts, grams, gath,
                  s_send, s_recv, g_send, g_recv, a_send, a_recv):
    me = lax.axis_index(axis)
    mine = lax.axis_index(other)
    chunk = x_ref.shape[0] // n

    barrier = pltpu.get_barrier_semaphore()
    for d in range(1, n):
        pl.semaphore_signal(barrier, inc=1, device_id={axis: lax.rem(me + d, n)}, device_id_type=MESH)
    for d in range(1, m):
        pl.semaphore_signal(barrier, inc=1, device_id={other: lax.rem(mine + d, m)}, device_id_type=MESH)
    pl.semaphore_wait(barrier, n + m - 2)

    scatter = []
    for d in range(1, n):
        peer = lax.rem(me + d, n)
        copy = pltpu.make_async_remote_copy(
            src_ref=x_ref.at[pl.ds(pl.multiple_of(peer * chunk, chunk), chunk), :],
            dst_ref=parts.at[d - 1],
            send_sem=s_send.at[d - 1],
            recv_sem=s_recv.at[d - 1],
            device_id={axis: peer},
            device_id_type=MESH,
        )
        copy.start()
        scatter.append(copy)
    modes = x_ref[pl.ds(pl.multiple_of(me * chunk, chunk), chunk), :]
    for d in range(1, n):
        scatter[d - 1].wait()
        modes = modes + parts[d - 1]

    grams[0] = lax.dot_general(
        modes, modes, NT, precision=full_precision, preferred_element_type=jnp.float32
    )
    sums = []
    for d in range(1, m):
        copy = pltpu.make_async_remote_copy(
            src_ref=grams.at[0],
            dst_ref=grams.at[d],
            send_sem=g_send.at[d - 1],
            recv_sem=g_recv.at[d - 1],
            device_id={other: lax.rem(mine + d, m)},
            device_id_type=MESH,
        )
        copy.start()
        sums.append(copy)
    gram = grams[0]
    for d in range(1, m):
        sums[d - 1].wait()
        gram = gram + grams[d]

    inverse = inverse_factor(gram)
    gath[0] = lax.dot_general(
        inverse, modes, NN, precision=full_precision, preferred_element_type=jnp.float32
    )
    gather = []
    for d in range(1, n):
        copy = pltpu.make_async_remote_copy(
            src_ref=gath.at[0],
            dst_ref=gath.at[d],
            send_sem=a_send.at[d - 1],
            recv_sem=a_recv.at[d - 1],
            device_id={axis: lax.rem(me + d, n)},
            device_id_type=MESH,
        )
        copy.start()
        gather.append(copy)
    out_ref[pl.ds(pl.multiple_of(me * chunk, chunk), chunk), :] = gath[0]
    for d in range(1, n):
        gather[d - 1].wait()
        owner = lax.rem(me + n - d, n)
        out_ref[pl.ds(pl.multiple_of(owner * chunk, chunk), chunk), :] = gath[d]


def reduce_normalize(partial, axis, other, number):
    scales, size, width = partial.shape
    n, m = lax.axis_size(axis), lax.axis_size(other)
    if n != scales:
        modes = lax.psum(partial, axis)
        gram = lax.psum(jnp.einsum("skm,slm->skl", modes, modes, precision=full_precision), other)
        lower = jnp.linalg.cholesky(gram)
        return lax.linalg.triangular_solve(lower, modes, left_side=True, lower=True)
    dma = pltpu.SemaphoreType.DMA
    flat = pl.pallas_call(
        functools.partial(reduce_kernel, axis, other, n, m),
        out_shape=jax.ShapeDtypeStruct((scales * size, width), jnp.float32),
        in_specs=[pl.BlockSpec(memory_space=pltpu.VMEM)],
        out_specs=pl.BlockSpec(memory_space=pltpu.VMEM),
        scratch_shapes=[
            pltpu.VMEM((n - 1, size, width), jnp.float32),
            pltpu.VMEM((m, size, size), jnp.float32),
            pltpu.VMEM((n, size, width), jnp.float32),
            dma((n - 1,)), dma((n - 1,)),
            dma((m - 1,)), dma((m - 1,)),
            dma((n - 1,)), dma((n - 1,)),
        ],
        compiler_params=pltpu.CompilerParams(collective_id=number, has_side_effects=True),
    )(partial.reshape(scales * size, width))
    return flat.reshape(scales, size, width)


def prior_of_rows(prior, row_tiles, first_row, row_pos, col_pos):
    rows, cols = lax.axis_size("row"), lax.axis_size("col")
    if rows == cols:
        total = jnp.where(row_pos == col_pos, prior, 0.0)
        for d in range(1, cols):
            pairs = [(r * cols + r, r * cols + (r + d) % cols) for r in range(rows)]
            moved = lax.ppermute(prior, ("row", "col"), pairs)
            total = jnp.where(col_pos == lax.rem(row_pos + d, cols), moved, total)
        return total
    everything = lax.all_gather(prior, "col", axis=0, tiled=True)
    return lax.dynamic_slice_in_dim(everything, first_row, row_tiles, 0)


def shards(covariance, prior, offsets, basis):
    scales, rows, cols = covariance.shape
    tile = prior.shape[2]
    reach = H * tile
    row_tiles, col_tiles = rows // tile, cols // tile
    row_pos, col_pos = lax.axis_index("row"), lax.axis_index("col")
    first_row, first_col = row_pos * row_tiles, col_pos * col_tiles

    slabs = []
    for s in range(scales):
        slabs.append(halos(covariance[s], "row", 0, reach))
    left_prior = prior_of_rows(prior, row_tiles, first_row, row_pos, col_pos)
    left_table = (lax.dynamic_slice_in_dim(offsets, first_row, row_tiles, 0) - first_row + H).reshape(-1)
    right_table = (lax.dynamic_slice_in_dim(offsets, first_col, col_tiles, 0) - first_col + H).reshape(-1)
    transposed = jnp.swapaxes(basis, 1, 2)

    whitened, parts = None, []
    for s in range(scales):
        before, after = slabs[s]
        if s:
            before, after, _ = lax.optimization_barrier((before, after, left))
        padded = jnp.concatenate(before + [covariance[s]] + after, axis=0)
        left = left_whiten(left_table, left_prior, padded, rows)
        before, after = halos(left, "col", 1, reach)
        widened = jnp.concatenate(before + [left] + after, axis=1)
        whitened, part = right_whiten(
            right_table, prior, widened, transposed[s], s, scales, cols, whitened
        )
        parts.append(part)

    current = reduce_normalize(jnp.stack(parts), "col", "row", 0)
    for sweep in range(1, ITERS):
        axis, other = ("row", "col") if sweep % 2 else ("col", "row")
        form = "skm,smn->skn" if sweep % 2 else "skn,smn->skm"
        partial = jnp.einsum(form, current, whitened, precision=lax.Precision.HIGH)
        current = reduce_normalize(partial, axis, other, sweep)
    return (whitened, jnp.swapaxes(current, 1, 2))


def solution(mesh):
    placed = (P("region", "row", "col"), P("col", None, None, None), P(), P("region", "col", None))
    return jax.shard_map(
        shards,
        mesh=mesh,
        in_specs=placed,
        out_specs=(P("region", "row", "col"), P("region", "col", None)),
        check_vma=False,
    )
```

```python
import functools
import jax
import jax.numpy as jnp
from jax import lax
from jax.experimental import pallas as pl
from jax.experimental.pallas import tpu as pltpu
from jax.sharding import PartitionSpec as P

H = 2
ITERS = 2


full_precision = lax.Precision.HIGHEST
MESH = pl.DeviceIdType.MESH
NN = (((1,), (0,)), ((), ()))
NT = (((1,), (1,)), ((), ()))


def halos(array, axis, dim, width):
    peers, length = lax.axis_size(axis), array.shape[dim]
    before, after = [], []
    done, step = 0, 1
    while done < width:
        take = min(length, width - done)
        last = lax.slice_in_dim(array, length - take, length, axis=dim)
        lead = lax.slice_in_dim(array, 0, take, axis=dim)
        before.insert(0, lax.ppermute(last, axis, [(i, i + step) for i in range(peers - step)]))
        after.append(lax.ppermute(lead, axis, [(i + step, i) for i in range(peers - step)]))
        done, step = done + take, step + 1
    return before, after


def halves(x):
    high = x.astype(jnp.bfloat16)
    return high, (x - high.astype(jnp.float32)).astype(jnp.bfloat16)


def product(a, b, dims):
    (da,), (db,) = dims[0]
    ah, al = zip(*map(halves, a))
    bh, bl = zip(*map(halves, b))
    left = jnp.concatenate(ah + ah + al, axis=da)
    right = jnp.concatenate(bh + bl + bh, axis=db)
    return lax.dot_general(left, right, dims, preferred_element_type=jnp.float32)


def left_kernel(slots, tab_ref, p_ref, *refs):
    out_ref = refs[-1]
    band = range(slots)
    out_ref[...] = product([p_ref[0, b] for b in band], [refs[b][...] for b in band], NN)


def left_whiten(table, prior, padded, rows):
    tiles, slots, tile, _ = prior.shape
    cols = padded.shape[1]

    def band_map(b, i, tab):
        return (tab[i * slots + b], 0)

    return pl.pallas_call(
        functools.partial(left_kernel, slots),
        out_shape=jax.ShapeDtypeStruct((rows, cols), jnp.float32),
        grid_spec=pltpu.PrefetchScalarGridSpec(
            num_scalar_prefetch=1,
            grid=(tiles,),
            in_specs=[pl.BlockSpec((1, slots, tile, tile), lambda i, tab: (i, 0, 0, 0))]
            + [pl.BlockSpec((tile, cols), functools.partial(band_map, b)) for b in range(slots)],
            out_specs=pl.BlockSpec((tile, cols), lambda i, tab: (i, 0)),
        ),
        cost_estimate=pl.CostEstimate(
            flops=6 * rows * slots * tile * cols, bytes_accessed=4 * rows * cols * 4, transcendentals=0
        ),
        name="left_whiten",
    )(table, prior, *([padded] * slots))


def right_kernel(slots, aliased, tab_ref, p_ref, cur_ref, *refs):
    out_ref, modes_ref = refs[slots + aliased], refs[slots + aliased + 1]
    band = range(slots)
    total = product([refs[b][...] for b in band], [p_ref[0, b] for b in band], NT)
    out_ref[0] = total
    part = product([cur_ref[...]], [total], NT)
    step = pl.program_id(0)

    @pl.when(step == 0)
    def _():
        modes_ref[...] = part

    @pl.when(step > 0)
    def _():
        modes_ref[...] += part


def right_whiten(table, prior, widened, current, scale, scales, cols, held):
    tiles, slots, tile, _ = prior.shape
    rows = widened.shape[0]
    modes = current.shape[0]

    def band_map(b, j, tab):
        return (0, tab[j * slots + b])

    aliased = 0 if held is None else 1
    in_specs = [
        pl.BlockSpec((1, slots, tile, tile), lambda j, tab: (j, 0, 0, 0)),
        pl.BlockSpec((modes, tile), lambda j, tab: (0, j)),
    ] + [pl.BlockSpec((rows, tile), functools.partial(band_map, b)) for b in range(slots)]
    args = [table, prior, current] + [widened] * slots
    aliases = {}
    if aliased:
        in_specs.append(pl.BlockSpec(memory_space=pl.ANY))
        aliases = {len(args): 0}
        args.append(held)
    return pl.pallas_call(
        functools.partial(right_kernel, slots, aliased),
        out_shape=(
            jax.ShapeDtypeStruct((scales, rows, cols), jnp.float32),
            jax.ShapeDtypeStruct((modes, rows), jnp.float32),
        ),
        grid_spec=pltpu.PrefetchScalarGridSpec(
            num_scalar_prefetch=1,
            grid=(tiles,),
            in_specs=in_specs,
            out_specs=[
                pl.BlockSpec((1, rows, tile), lambda j, tab: (scale, 0, j)),
                pl.BlockSpec((modes, rows), lambda j, tab: (0, 0)),
            ],
        ),
        input_output_aliases=aliases,
        cost_estimate=pl.CostEstimate(
            flops=6 * rows * slots * tile * cols, bytes_accessed=4 * rows * cols * 4, transcendentals=0
        ),
        name="right_whiten",
    )(*args)


def inverse_factor(gram):
    size = gram.shape[0]
    shape = (size, 2 * size)
    sub = lax.broadcasted_iota(jnp.int32, shape, 0)
    lane = lax.broadcasted_iota(jnp.int32, shape, 1)
    unit = jnp.where(lane == sub + size, 1.0, 0.0).astype(jnp.float32)
    start = jnp.concatenate([gram, unit[:, size:]], axis=1)

    def step(j, a):
        col = jnp.sum(jnp.where(lane == j, a, 0.0), axis=1, keepdims=True)
        row = jnp.sum(jnp.where(sub == j, a, 0.0), axis=0, keepdims=True)
        pivot = jnp.sum(jnp.where(sub[:, :1] == j, col, 0.0), axis=0, keepdims=True)
        return jnp.where(sub > j, a - (col * (1.0 / pivot)) * row, a)

    a = lax.fori_loop(0, size, step, start)
    pivots = jnp.sum(jnp.where(lane == sub, a, 0.0), axis=1, keepdims=True)
    return (a / jnp.sqrt(pivots))[:, size:]


def reduce_kernel(axis, other, n, m, x_ref, out_ref, parts, grams, gath,
                  s_send, s_recv, g_send, g_recv, a_send, a_recv):
    me = lax.axis_index(axis)
    mine = lax.axis_index(other)
    chunk = x_ref.shape[0] // n

    barrier = pltpu.get_barrier_semaphore()
    for d in range(1, n):
        pl.semaphore_signal(barrier, inc=1, device_id={axis: lax.rem(me + d, n)}, device_id_type=MESH)
    for d in range(1, m):
        pl.semaphore_signal(barrier, inc=1, device_id={other: lax.rem(mine + d, m)}, device_id_type=MESH)
    pl.semaphore_wait(barrier, n + m - 2)

    scatter = []
    for d in range(1, n):
        peer = lax.rem(me + d, n)
        copy = pltpu.make_async_remote_copy(
            src_ref=x_ref.at[pl.ds(pl.multiple_of(peer * chunk, chunk), chunk), :],
            dst_ref=parts.at[d - 1],
            send_sem=s_send.at[d - 1],
            recv_sem=s_recv.at[d - 1],
            device_id={axis: peer},
            device_id_type=MESH,
        )
        copy.start()
        scatter.append(copy)
    modes = x_ref[pl.ds(pl.multiple_of(me * chunk, chunk), chunk), :]
    for d in range(1, n):
        scatter[d - 1].wait()
        modes = modes + parts[d - 1]

    grams[0] = lax.dot_general(
        modes, modes, NT, precision=full_precision, preferred_element_type=jnp.float32
    )
    sums = []
    for d in range(1, m):
        copy = pltpu.make_async_remote_copy(
            src_ref=grams.at[0],
            dst_ref=grams.at[d],
            send_sem=g_send.at[d - 1],
            recv_sem=g_recv.at[d - 1],
            device_id={other: lax.rem(mine + d, m)},
            device_id_type=MESH,
        )
        copy.start()
        sums.append(copy)
    gram = grams[0]
    for d in range(1, m):
        sums[d - 1].wait()
        gram = gram + grams[d]

    inverse = inverse_factor(gram)
    gath[0] = lax.dot_general(
        inverse, modes, NN, precision=full_precision, preferred_element_type=jnp.float32
    )
    gather = []
    for d in range(1, n):
        copy = pltpu.make_async_remote_copy(
            src_ref=gath.at[0],
            dst_ref=gath.at[d],
            send_sem=a_send.at[d - 1],
            recv_sem=a_recv.at[d - 1],
            device_id={axis: lax.rem(me + d, n)},
            device_id_type=MESH,
        )
        copy.start()
        gather.append(copy)
    out_ref[pl.ds(pl.multiple_of(me * chunk, chunk), chunk), :] = gath[0]
    for d in range(1, n):
        gather[d - 1].wait()
        owner = lax.rem(me + n - d, n)
        out_ref[pl.ds(pl.multiple_of(owner * chunk, chunk), chunk), :] = gath[d]


def reduce_normalize(partial, axis, other, number):
    scales, size, width = partial.shape
    n, m = lax.axis_size(axis), lax.axis_size(other)
    if n != scales:
        modes = lax.psum(partial, axis)
        gram = lax.psum(jnp.einsum("skm,slm->skl", modes, modes, precision=full_precision), other)
        lower = jnp.linalg.cholesky(gram)
        return lax.linalg.triangular_solve(lower, modes, left_side=True, lower=True)
    dma = pltpu.SemaphoreType.DMA
    flat = pl.pallas_call(
        functools.partial(reduce_kernel, axis, other, n, m),
        out_shape=jax.ShapeDtypeStruct((scales * size, width), jnp.float32),
        in_specs=[pl.BlockSpec(memory_space=pltpu.VMEM)],
        out_specs=pl.BlockSpec(memory_space=pltpu.VMEM),
        scratch_shapes=[
            pltpu.VMEM((n - 1, size, width), jnp.float32),
            pltpu.VMEM((m, size, size), jnp.float32),
            pltpu.VMEM((n, size, width), jnp.float32),
            dma((n - 1,)), dma((n - 1,)),
            dma((m - 1,)), dma((m - 1,)),
            dma((n - 1,)), dma((n - 1,)),
        ],
        compiler_params=pltpu.CompilerParams(collective_id=number, has_side_effects=True),
    )(partial.reshape(scales * size, width))
    return flat.reshape(scales, size, width)


def prior_of_rows(prior, row_tiles, first_row, row_pos, col_pos):
    rows, cols = lax.axis_size("row"), lax.axis_size("col")
    if rows == cols:
        total = jnp.where(row_pos == col_pos, prior, 0.0)
        for d in range(1, cols):
            pairs = [(r * cols + r, r * cols + (r + d) % cols) for r in range(rows)]
            moved = lax.ppermute(prior, ("row", "col"), pairs)
            total = jnp.where(col_pos == lax.rem(row_pos + d, cols), moved, total)
        return total
    everything = lax.all_gather(prior, "col", axis=0, tiled=True)
    return lax.dynamic_slice_in_dim(everything, first_row, row_tiles, 0)


def shards(covariance, prior, offsets, basis):
    scales, rows, cols = covariance.shape
    tile = prior.shape[2]
    reach = H * tile
    row_tiles, col_tiles = rows // tile, cols // tile
    row_pos, col_pos = lax.axis_index("row"), lax.axis_index("col")
    first_row, first_col = row_pos * row_tiles, col_pos * col_tiles

    slabs = []
    for s in range(scales):
        slabs.append(halos(covariance[s], "row", 0, reach))
    left_prior = prior_of_rows(prior, row_tiles, first_row, row_pos, col_pos)
    left_table = (lax.dynamic_slice_in_dim(offsets, first_row, row_tiles, 0) - first_row + H).reshape(-1)
    right_table = (lax.dynamic_slice_in_dim(offsets, first_col, col_tiles, 0) - first_col + H).reshape(-1)
    transposed = jnp.swapaxes(basis, 1, 2)

    whitened, parts = None, []
    for s in range(scales):
        before, after = slabs[s]
        if s:
            before, after, _ = lax.optimization_barrier((before, after, left))
        padded = jnp.concatenate(before + [covariance[s]] + after, axis=0)
        left = left_whiten(left_table, left_prior, padded, rows)
        before, after = halos(left, "col", 1, reach)
        widened = jnp.concatenate(before + [left] + after, axis=1)
        whitened, part = right_whiten(
            right_table, prior, widened, transposed[s], s, scales, cols, whitened
        )
        parts.append(part)

    current = reduce_normalize(jnp.stack(parts), "col", "row", 0)
    for sweep in range(1, ITERS):
        axis, other = ("row", "col") if sweep % 2 else ("col", "row")
        form = "skm,smn->skn" if sweep % 2 else "skn,smn->skm"
        partial = jnp.einsum(form, current, whitened, precision=lax.Precision.HIGH)
        current = reduce_normalize(partial, axis, other, sweep)
    return (whitened, jnp.swapaxes(current, 1, 2))


def solution(mesh):
    placed = (P("region", "row", "col"), P("col", None, None, None), P(), P("region", "col", None))
    return jax.shard_map(
        shards,
        mesh=mesh,
        in_specs=placed,
        out_specs=(P("region", "row", "col"), P("region", "col", None)),
        check_vma=False,
    )
```
